512 devices in a mesh: sub: 128 (over z, x, core), tile: 4 (over y).
Axes of the slice: x: 4, y: 4, z: 16, core: 2. Of those that a mesh axis runs over, the one named last changes fastest.
Arguments:
- ray_cot: float32 [4, 4, 32768], P(None, 'tile', 'sub'), may hold values from -6 to 6
- ray_lists: int32 [4, 32768, 8], P('tile', 'sub'), may hold values from 0 to 127, all different within a row; in each aligned block of 256 rows (0 to 255, 256 to 511, ..., all dimensions but the last counted through in order) at most 32 rows name the same one
- geometry: float32 [7, 262144], P(None, 'sub'), may hold values from -1024 to 1024, as said below
- sh_coef: float32 [48, 262144], P(None, 'sub'), may hold values from -1.8 to 1.8
- view_angles: float32 [4, 2], replicated, may hold values from -3.140625 to 3.140625
- block_ids: int32 [128, 4, 4], P('sub', 'tile'), may hold values from 0 to 15, as said below
- block_counts: int32 [128, 4], P('sub', 'tile'), may hold values from 1 to 4, as said below
Outputs:
- geo_grad: float32 [7, 262144], P(None, 'sub')
- sh_grad: float32 [48, 262144], P(None, 'sub')
The draws below stay inside these ranges and needn't reach their ends.
Inputs may be any that keep to these rules, and one draw needn't show every extreme that they name: `ray_lists`: each row names 8 different subspaces, in the order in which the ray meets them; among the rows of one device no subspace is named more than 32 times, a bound that some block reaches. `block_ids`: each list holds 4 different resident block numbers. `block_counts`: both ends are reached in every draw. `geometry`: rows 0 and 1 are a Gaussian's centre in pixels (column, row); rows 2 to 4 are A, B, C of a positive definite inverse covariance [[A, B], [B, C]]; row 5 is an opacity between 0.05 and 0.9; row 6 is a depth between 0.5 and 2.
All inputs are finite; a program needn't handle non-finite values.
Results may differ from the reference program's by a relative error of at most 0.0003.
Values sent between devices are 32-bit elements; how exact they have to be, the bound alone decides.
A program may use at most 64 MiB of HBM per device.

```python
import math
import jax
import jax.numpy as jnp
import numpy as np
from jax import lax

RAY_DEV = 256
IMG_W = 1024
BLOCK = 128
NLIST = 4
NBLK = 16
LISTED = 8
SH_ROWS = 48
GEO_ROWS = 7
SUBS = 128
TILES = 4
RAYS_TILE = 32768
CAP = 32
ROWS = 32
GAUSS_DEV = 2048
GAUSS = 262144
N_SUB = 128


def draw_geometry(key, part):
    subkeys = jax.random.split(key, 7)
    gaussians = GAUSS
    spread = 3216.0 / (IMG_W * ROWS)
    mean_x = jax.random.uniform(subkeys[0], (gaussians,), jnp.float32, 0.0, 1.0 * IMG_W)
    mean_y = jax.random.uniform(subkeys[1], (gaussians,), jnp.float32, -0.5, ROWS - 0.5)
    conic_a = spread * jnp.exp(jax.random.uniform(subkeys[2], (gaussians,), jnp.float32, -0.6931, 0.6931))
    conic_c = spread * jnp.exp(jax.random.uniform(subkeys[3], (gaussians,), jnp.float32, -0.6931, 0.6931))
    relation = jax.random.uniform(subkeys[4], (gaussians,), jnp.float32, -0.6, 0.6)
    opacity = jax.random.uniform(subkeys[5], (gaussians,), jnp.float32, 0.05, 0.9)
    depth = jax.random.uniform(subkeys[6], (gaussians,), jnp.float32, 0.5, 2.0)
    conic_b = relation * jnp.sqrt(conic_a * conic_c)
    return jnp.stack([mean_x, mean_y, conic_a, conic_b, conic_c, opacity, depth]).astype(jnp.float32)


def draw_block_ids(key, part):
    subkeys = jax.random.split(key, SUBS * TILES)
    orders = jax.vmap(lambda single: jax.random.permutation(single, NBLK)[:NLIST])(subkeys)
    return orders.reshape(SUBS, TILES, NLIST).astype(jnp.int32)


def draw_block_counts(key, part):
    key_first, key_second, key_third = jax.random.split(key, 3)
    pair_count = SUBS * TILES
    counts_flat = jax.random.randint(key_first, (pair_count,), 1, NLIST + 1)
    fullest = jax.random.randint(key_second, (), 0, pair_count)
    emptiest = (fullest + 1 + jax.random.randint(key_third, (), 0, pair_count - 1)) % pair_count
    counts_flat = counts_flat.at[fullest].set(NLIST).at[emptiest].set(1)
    return counts_flat.reshape(SUBS, TILES).astype(jnp.int32)


def steps_of(rng, dims, cuts, least, high):
    gain, own = 1.0, jax.random.fold_in(rng, 6)
    for axis_at, parts in cuts:
        draws = jnp.exp(jax.random.uniform(jax.random.fold_in(own, axis_at), (parts,), jnp.float32, least / len(cuts), high / len(cuts)))
        gain = gain * jnp.repeat(draws, dims[axis_at] // parts).reshape([-1 if axis == axis_at else 1 for axis in range(len(dims))])
    return gain


def shared_out(rng, own, number, rows, number_of, top, limit, slope):
    sequence = jax.random.permutation(rng, number_of)
    heavy_load, ordinary = load_shares(number_of, rows * top, limit, slope, True), load_shares(number_of, rows * top, limit, slope, False)
    places = jnp.arange(number_of)

    def named(lengths, rotation):
        used = int((lengths > 0).sum())
        fixed = max(1, used // 4)
        passed = fixed + (places - fixed + rotation * (used - fixed)) % max(1, number_of - fixed)
        return jnp.zeros((number_of,), jnp.int32).at[sequence[jnp.where(places < fixed, places, passed)]].set(jnp.asarray(lengths, jnp.int32))

    lengths = jnp.where(number % 4 == 0, named(heavy_load, number // 4), named(ordinary, number - number // 4 - 1))
    mixed = jax.random.permutation(jax.random.fold_in(own, 3), number_of)
    source_of, receiver = mixed[0:number_of // 2 * 2:2], mixed[1:number_of // 2 * 2:2]
    slack = jnp.minimum(lengths[source_of] - 1, limit - lengths[receiver]) // 2
    slack = jnp.where((source_of == sequence[0]) | (receiver == sequence[0]) | (lengths[receiver] == 0), 0, jnp.maximum(slack, 0))
    passed = jax.random.randint(jax.random.fold_in(own, 4), (number_of // 2,), 0, 1 << 20) % (slack + 1)
    lengths = lengths.at[source_of].add(-passed).at[receiver].add(passed)
    labels = jnp.searchsorted(jnp.cumsum(lengths), jnp.arange(rows * top), side="right").astype(jnp.int32)
    grid = labels.reshape(top, rows).T
    grid = grid[jax.random.permutation(jax.random.fold_in(own, 1), rows)]
    rotation = jax.random.randint(jax.random.fold_in(own, 2), (rows, 1), 0, top)
    return jnp.take_along_axis(grid, (jnp.arange(top)[None, :] + rotation) % top, axis=1)


def load_shares(number_of, total, reach, skew, full):
    portions = [(1 << 20) // math.isqrt(standing ** skew) + 1 for standing in range(1, number_of + 1)]
    largest = reach if full else min(reach, max(-(-total // number_of), total * portions[0] // sum(portions)))
    least = 1 if total - largest >= number_of - 1 else 0
    given, surplus = [largest] + [least] * (number_of - 1), total - largest - least * (number_of - 1)
    while surplus > 0:
        free = [i for i in range(1, number_of) if given[i] < largest] or [i for i in range(1, number_of) if given[i] < reach]
        whole, budget = sum([portions[i] for i in free]), surplus
        for i in free:
            more = min(reach - given[i], max(1, budget * portions[i] // whole), surplus)
            given[i] = given[i] + more
            surplus = surplus - more
    return np.array(given)


def noise(stream_key, dims, width, most, pieces=(), kind=jnp.bfloat16):
    values = width * jax.random.normal(stream_key, dims, jnp.float32)
    if pieces:
        values = values * steps_of(stream_key, dims, pieces, -0.22, 0.18)
    return jnp.clip(values, -most, most).astype(kind)


def setup_inputs(seed: int = 0) -> dict:
    streams_of = jax.random.split(jax.random.key(seed), 8)
    ray_cot = noise(streams_of[0], (4, TILES, RAYS_TILE), 1.0, 6.0, ((1, 4), (2, 128)), jnp.float32)
    ray_lists_keys = jax.random.split(jax.random.fold_in(streams_of[1], 1), TILES * RAYS_TILE // RAY_DEV)
    ray_lists_turns = jax.random.permutation(jax.random.fold_in(streams_of[1], 3), TILES * RAYS_TILE // RAY_DEV)
    ray_lists = jax.vmap(lambda own, number: shared_out(jax.random.fold_in(streams_of[1], 2), own, number, RAY_DEV, SUBS, LISTED, CAP, 2))(ray_lists_keys, ray_lists_turns).reshape((TILES, RAYS_TILE, LISTED))
    geometry = draw_geometry(jax.random.fold_in(streams_of[7], 71), 0)
    sh_coef = noise(streams_of[3], (SH_ROWS, GAUSS), 0.3, 1.8, ((1, 128),), jnp.float32)
    view_angles = jnp.clip(jax.random.uniform(streams_of[4], (TILES, 2), jnp.float32, -3.140625, 3.140625), -3.140625, 3.140625)
    block_ids = draw_block_ids(jax.random.fold_in(streams_of[7], 71), 0)
    block_counts = draw_block_counts(jax.random.fold_in(streams_of[7], 71), 0)
    return dict(ray_cot=ray_cot, ray_lists=ray_lists, geometry=geometry, sh_coef=sh_coef, view_angles=view_angles, block_ids=block_ids, block_counts=block_counts)


distant = -10000.0
highest = lax.Precision.HIGHEST

def view_basis(angle_pair):
    azimuth = angle_pair[0]
    elevation = angle_pair[1]
    along_x = jnp.cos(elevation) * jnp.cos(azimuth)
    along_y = jnp.cos(elevation) * jnp.sin(azimuth)
    along_z = jnp.sin(elevation)
    square_x = along_x * along_x
    square_y = along_y * along_y
    square_z = along_z * along_z
    terms = [0.28209479177387814 * jnp.ones_like(along_x), -0.4886025119029199 * along_y, 0.4886025119029199 * along_z, -0.4886025119029199 * along_x, 1.0925484305920792 * along_x * along_y, -1.0925484305920792 * along_y * along_z, 0.31539156525252005 * (2.0 * square_z - square_x - square_y), -1.0925484305920792 * along_x * along_z, 0.5462742152960396 * (square_x - square_y), -0.5900435899266435 * along_y * (3.0 * square_x - square_y), 2.890611442640554 * along_x * along_y * along_z, -0.4570457994644658 * along_y * (4.0 * square_z - square_x - square_y), 0.3731763325901154 * along_z * (2.0 * square_z - 3.0 * square_x - 3.0 * square_y), -0.4570457994644658 * along_x * (4.0 * square_z - square_x - square_y), 1.445305721320277 * along_z * (square_x - square_y), -0.5900435899266435 * along_x * (square_x - 3.0 * square_y)]
    return jnp.stack(terms)

def colours(sh_coef, harmonics):
    table = sh_coef.reshape(16, 3, -1)
    return 0.5 + jnp.einsum('k,kcg->cg', harmonics, table, precision=highest)

def render(block_geometry, block_features, block_active, coords):
    slot_count = coords.shape[1]
    block_size = block_geometry.shape[2]
    lower = (jnp.arange(block_size, dtype=jnp.int32)[:, None] > jnp.arange(block_size, dtype=jnp.int32)[None, :]).astype(jnp.float32)

    def advance(running, inputs):
        gathered, passing = running
        shapes, tinted, active = inputs
        offset_x = coords[0][None, :] - shapes[0][:, None]
        offset_y = coords[1][None, :] - shapes[1][:, None]
        exponent = shapes[2][:, None] * offset_x * offset_x + 2.0 * shapes[3][:, None] * offset_x * offset_y + shapes[4][:, None] * offset_y * offset_y
        alphas = active * shapes[5][:, None] * jnp.exp(-0.5 * exponent)
        log_keep = jnp.log1p(-alphas)
        before = jnp.dot(lower, log_keep, precision=highest)
        weights = alphas * passing[None, :] * jnp.exp(before)
        gathered = gathered + jnp.dot(tinted, weights, precision=highest)
        passing = passing * jnp.exp(lax.optimization_barrier(jnp.sum(log_keep, axis=0)))
        return ((gathered, passing), None)
    initial = (jnp.zeros((4, slot_count), jnp.float32), jnp.ones((slot_count,), jnp.float32))
    scanned = (jnp.transpose(block_geometry, (1, 0, 2)), jnp.transpose(block_features, (1, 0, 2)), block_active)
    (gathered, passing), _ = lax.scan(jax.checkpoint(advance), initial, scanned)
    return jnp.concatenate([gathered, passing[None, :]], axis=0)

def compose(entries):
    result = jnp.zeros_like(entries[:4, :, 0])
    carried = jnp.ones_like(entries[4, :, 0])
    for column in range(entries.shape[2]):
        result = result + carried[None, :] * entries[:4, :, column]
        carried = carried * entries[4, :, column]
    return result

def reference(ray_cot, ray_lists, geometry, sh_coef, view_angles, block_ids, block_counts):
    entries_dev = RAY_DEV * LISTED
    subspace_ids = jnp.arange(SUBS, dtype=jnp.int32)

    def total_loss(geometry, sh_coef):
        loss_sum = jnp.zeros((), jnp.float32)
        for view_index in range(TILES):
            harmonics = view_basis(view_angles[view_index])
            features = jnp.concatenate([colours(sh_coef, harmonics), geometry[6:7]], axis=0)
            targets = ray_lists[view_index].reshape(N_SUB, entries_dev).astype(jnp.int32)
            matches = (targets[:, :, None] == subspace_ids[None, None, :]).astype(jnp.int32)
            entry_rank = lax.optimization_barrier(jnp.sum((jnp.cumsum(matches, axis=1) - matches) * matches, axis=2)).astype(jnp.int32)
            sources = jnp.broadcast_to(jnp.arange(N_SUB, dtype=jnp.int32)[:, None], targets.shape)
            ray_index = jnp.arange(RAYS_TILE, dtype=jnp.int32)
            pixels = jnp.stack([(ray_index % IMG_W).astype(jnp.float32), (ray_index // IMG_W).astype(jnp.float32)])
            pixel_entries = jnp.repeat(pixels, LISTED, axis=1).reshape(2, N_SUB, entries_dev)
            queries = jnp.full((2, SUBS, N_SUB, CAP), distant, jnp.float32).at[:, targets, sources, entry_rank].set(pixel_entries)

            def one_subspace(subspace):
                chosen = block_ids[subspace, view_index].astype(jnp.int32)
                start_col = (subspace * GAUSS_DEV).astype(jnp.int32)
                resident_geo = lax.dynamic_slice_in_dim(geometry, start_col, GAUSS_DEV, 1).reshape(GEO_ROWS, NBLK, BLOCK)
                resident_feat = lax.dynamic_slice_in_dim(features, start_col, GAUSS_DEV, 1).reshape(4, NBLK, BLOCK)
                active = (jnp.arange(NLIST, dtype=jnp.int32) < block_counts[subspace, view_index]).astype(jnp.float32)
                local_queries = lax.dynamic_index_in_dim(queries, subspace, 1, keepdims=False).reshape(2, N_SUB * CAP)
                return render(resident_geo[:, chosen], resident_feat[:, chosen], active, local_queries)
            partials = lax.map(one_subspace, subspace_ids).reshape(SUBS, 5, N_SUB, CAP)
            picked = partials[targets, :, sources, entry_rank]
            picked = jnp.transpose(picked.reshape(RAYS_TILE, LISTED, 5), (2, 0, 1))
            loss_sum = loss_sum + jnp.sum(compose(picked) * ray_cot[:, view_index, :])
        return loss_sum
    geo_grad, sh_grad = jax.grad(total_loss, argnums=(0, 1))(geometry, sh_coef)
    return (geo_grad, sh_grad)
```

```python
import jax
import jax.numpy as jnp
from jax import lax
from jax.experimental import pallas as pl
from jax.experimental.pallas import tpu as pltpu
from jax.sharding import PartitionSpec as P

NZ, NX, NC, NT = 16, 4, 2, 4
PLANE = NX * NC
BLOCK, NLIST, LISTED, RAYS = 128, 4, 8, 256
LIVE = NLIST * BLOCK
LOG2E = 1.4426950408889634
f32, i32, bf16 = jnp.float32, jnp.int32, jnp.bfloat16
highest = lax.Precision.HIGHEST
UF, UB = 4, 8


def iota(shape, axis):
    return lax.broadcasted_iota(i32, shape, axis)


def take(table, index):
    return jnp.take_along_axis(table, index, axis=1, mode="promise_in_bounds")


def group_swap(tiles):
    lane = iota((8, 128), 1)
    low = lane < 64
    even = (lane // 32) % 2 == 0
    a, b, c, d = tiles
    a, c = jnp.where(low, a, pltpu.roll(c, 64, 1)), jnp.where(low, pltpu.roll(a, 64, 1), c)
    b, d = jnp.where(low, b, pltpu.roll(d, 64, 1)), jnp.where(low, pltpu.roll(b, 64, 1), d)
    a, b = jnp.where(even, a, pltpu.roll(b, 32, 1)), jnp.where(even, pltpu.roll(a, 96, 1), b)
    c, d = jnp.where(even, c, pltpu.roll(d, 32, 1)), jnp.where(even, pltpu.roll(c, 96, 1), d)
    return a, b, c, d


def pair_merge(first, second):
    low = iota((8, 128), 1) < 64
    return (
        jnp.where(low, first, pltpu.roll(second, 64, 1)),
        jnp.where(low, pltpu.roll(first, 64, 1), second),
    )


def harmonic_rows(angles):
    shape = (8 * NT, 128)
    view = iota(shape, 0) // 8
    row = iota(shape, 1)
    azimuth = jnp.zeros(shape, f32)
    elevation = jnp.zeros(shape, f32)
    for v in range(NT):
        azimuth = jnp.where(view == v, angles[v, 0], azimuth)
        elevation = jnp.where(view == v, angles[v, 1], elevation)
    x = jnp.cos(elevation) * jnp.cos(azimuth)
    y = jnp.cos(elevation) * jnp.sin(azimuth)
    z = jnp.sin(elevation)
    xx, yy, zz = x * x, y * y, z * z
    terms = [
        0.28209479177387814 * jnp.ones_like(x),
        -0.4886025119029199 * y,
        0.4886025119029199 * z,
        -0.4886025119029199 * x,
        1.0925484305920792 * x * y,
        -1.0925484305920792 * y * z,
        0.31539156525252005 * (2.0 * zz - xx - yy),
        -1.0925484305920792 * x * z,
        0.5462742152960396 * (xx - yy),
        -0.5900435899266435 * y * (3.0 * xx - yy),
        2.890611442640554 * x * y * z,
        -0.4570457994644658 * y * (4.0 * zz - xx - yy),
        0.3731763325901154 * z * (2.0 * zz - 3.0 * xx - 3.0 * yy),
        -0.4570457994644658 * x * (4.0 * zz - xx - yy),
        1.445305721320277 * z * (xx - yy),
        -0.5900435899266435 * x * (xx - 3.0 * yy),
    ]
    out = jnp.zeros(shape, f32)
    for k, term in enumerate(terms):
        out = jnp.where(row // 3 == k, term, out)
    return jnp.where((row % 3 == iota(shape, 0) % 8) & (row < 48), out, 0.0)


def kernel(
    angles, ids, counts, cot_ref, lists_ref, geo_hbm, sh_hbm,
    pay_out, har_out,
    geo_s, sh_s, cum_s, rank_s, slot_s,
    zs_i, zr_i, zs_c, zr_c, xs_i, xr_i, xs_c, xr_c,
    xs_2, xr_2, zs_2, zr_2, zs_3, zr_3, xs_3, xr_3,
    rows_s, alpha_s, weight_s, tint_s, acc_s, red_s, cot_s, pay_s, pay_r,
    zsend, zrecv, xsend, xrecv, ysend, yrecv, lsem,
):
    me = lax.axis_index("sub")
    view = lax.axis_index("tile")
    mz = me // PLANE
    mp = me % PLANE

    def far(i):
        return (mz + 8 + ((i + 1) // 2) * (1 - 2 * (i % 2)) + NZ) % NZ

    barrier = pltpu.get_barrier_semaphore()

    def greet_z(i, c):
        pl.semaphore_signal(barrier, inc=1, device_id={"sub": far(i) * PLANE + mp})
        return c

    def greet_p(i, c):
        pl.semaphore_signal(barrier, inc=1, device_id={"sub": mz * PLANE + (mp + 1 + i) % PLANE})
        return c

    def greet_y(i, c):
        pl.semaphore_signal(barrier, inc=1, device_id={"tile": (view + 1 + i) % NT})
        return c

    lax.fori_loop(0, NZ - 1, greet_z, 0)
    lax.fori_loop(0, PLANE - 1, greet_p, 0)
    lax.fori_loop(0, NT - 1, greet_y, 0)

    geo_copy = pltpu.make_async_copy(geo_hbm, geo_s, lsem.at[0])
    sh_copy = pltpu.make_async_copy(sh_hbm, sh_s, lsem.at[1])
    geo_copy.start()
    sh_copy.start()

    def z_copy(src, dst, phase, other):
        return pltpu.make_async_remote_copy(
            src_ref=src.at[:, other, :],
            dst_ref=dst.at[:, mz, :],
            send_sem=zsend.at[phase, other],
            recv_sem=zrecv.at[phase, mz],
            device_id={"sub": other * PLANE + mp},
        )

    def z_start(src, dst, phase):
        pltpu.make_async_copy(src.at[:, mz, :], dst.at[:, mz, :], zrecv.at[phase, mz]).start()

        def go(i, c):
            z_copy(src, dst, phase, far(i)).start()
            return c

        lax.fori_loop(0, NZ - 1, go, 0)

    def z_wait(src, dst, phase):
        pltpu.make_async_copy(src.at[:, mz, :], dst.at[:, mz, :], zrecv.at[phase, mz]).wait()

        def go(i, c):
            other = (mz + 1 + i) % NZ
            pltpu.make_async_remote_copy(
                src_ref=src.at[:, other, :],
                dst_ref=dst.at[:, other, :],
                send_sem=zsend.at[phase, other],
                recv_sem=zrecv.at[phase, other],
                device_id={"sub": other * PLANE + mp},
            ).wait_recv()
            return c

        lax.fori_loop(0, NZ - 1, go, 0)

    def z_drain(src, dst, phase):
        def go(i, c):
            z_copy(src, dst, phase, (mz + 1 + i) % NZ).wait_send()
            return c

        lax.fori_loop(0, NZ - 1, go, 0)

    def x_copy(src, dst, phase, other):
        return pltpu.make_async_remote_copy(
            src_ref=src.at[other],
            dst_ref=dst.at[mp],
            send_sem=xsend.at[phase, other],
            recv_sem=xrecv.at[phase, mp],
            device_id={"sub": mz * PLANE + other},
        )

    def x_start(src, dst, phase):
        pltpu.make_async_copy(src.at[mp], dst.at[mp], xrecv.at[phase, mp]).start()

        def go(i, c):
            x_copy(src, dst, phase, (mp + 1 + i) % PLANE).start()
            return c

        lax.fori_loop(0, PLANE - 1, go, 0)

    def x_wait(src, dst, phase):
        pltpu.make_async_copy(src.at[mp], dst.at[mp], xrecv.at[phase, mp]).wait()

        def go(i, c):
            other = (mp + 1 + i) % PLANE
            pltpu.make_async_remote_copy(
                src_ref=src.at[other],
                dst_ref=dst.at[other],
                send_sem=xsend.at[phase, other],
                recv_sem=xrecv.at[phase, other],
                device_id={"sub": mz * PLANE + other},
            ).wait_recv()
            return c

        lax.fori_loop(0, PLANE - 1, go, 0)

    def x_drain(src, dst, phase):
        def go(i, c):
            x_copy(src, dst, phase, (mp + 1 + i) % PLANE).wait_send()
            return c

        lax.fori_loop(0, PLANE - 1, go, 0)

    lists = lists_ref[...]
    row = iota((128, RAYS), 0)
    named = (row % 16) * 8 + ((row // 16) % 2) * 4 + row // 32
    hit = jnp.zeros((128, RAYS), f32)
    for k in range(LISTED):
        hit = jnp.where(lists[k : k + 1, :] == named, 1.0, hit)
    upper = jnp.where(iota((RAYS, RAYS), 0) <= iota((RAYS, RAYS), 1), 1.0, 0.0).astype(bf16)
    cum = jnp.dot(hit.astype(bf16), upper, preferred_element_type=f32)
    cum_s[...] = cum
    rank_s[...] = jnp.minimum((cum - hit).astype(i32), 31)

    lane = iota((32, 128), 1)
    group = lane // 32
    want = (lane % 32).astype(f32)
    spot = jnp.zeros((32, 128), i32)
    half = jnp.zeros((32, 128), i32)
    valid = jnp.zeros((32, 128), i32)
    for q in range(4):
        left = cum_s[32 * q : 32 * q + 32, 0:128]
        right = cum_s[32 * q : 32 * q + 32, 128:256]
        in_right = left[:, 127:128] <= want
        pos = jnp.zeros((32, 128), i32)
        for step in (64, 32, 16, 8, 4, 2, 1):
            probe = pos + (step - 1)
            seen = jnp.where(in_right, take(right, probe), take(left, probe))
            pos = jnp.where(seen <= want, pos + step, pos)
        here = group == q
        spot = jnp.where(here, pos, spot)
        half = jnp.where(here & in_right, 1, half)
        valid = jnp.where(here & (want < right[:, 127:128]), 1, valid)
    slot_s[0] = spot
    slot_s[1] = half
    slot_s[2] = valid
    index = (spot + 128 * half).astype(f32)
    for h in range(2):
        zs_i[h] = index[16 * h : 16 * h + 16, :]
    for j in range(4):
        left = jnp.broadcast_to(cot_ref[j : j + 1, 0:128], (32, 128))
        right = jnp.broadcast_to(cot_ref[j : j + 1, 128:256], (32, 128))
        picked = jnp.where(half == 1, take(right, spot), take(left, spot))
        for h in range(2):
            zs_c[2 * j + h] = picked[16 * h : 16 * h + 16, :]

    pl.semaphore_wait(barrier, NZ - 1 + PLANE - 1 + NT - 1)
    z_start(zs_i, zr_i, 0)
    z_start(zs_c, zr_c, 1)

    harmonics = harmonic_rows(angles)
    har_out[...] = harmonics
    cot_s[0:32, :] = harmonics
    geo_copy.wait()
    sh_copy.wait()
    own = cot_s[pl.ds(pl.multiple_of(view * 8, 8), 8), :]
    for l in range(NLIST):
        chosen = jnp.full((1, BLOCK), ids[l], i32)
        block = geo_s[:, 0:BLOCK]
        coef = sh_s[:, 0:BLOCK]
        for b in range(1, geo_s.shape[1] // BLOCK):
            match = chosen == b
            block = jnp.where(match, geo_s[:, b * BLOCK : (b + 1) * BLOCK], block)
            coef = jnp.where(match, sh_s[:, b * BLOCK : (b + 1) * BLOCK], coef)
        colour = 0.5 + jnp.dot(own[:, 0:48], coef, precision=highest)
        live = jnp.full((1, BLOCK), counts[0], i32) > l
        fade = jnp.where(live, jnp.log(block[5:6]) * LOG2E, -1e30)
        rows = jnp.concatenate(
            [
                block[0:2],
                block[2:3] * (-0.5 * LOG2E),
                block[3:4] * (-LOG2E),
                block[4:5] * (-0.5 * LOG2E),
                fade,
                colour[0:3],
                block[6:7],
                jnp.zeros((6, BLOCK), f32),
            ],
            axis=0,
        )
        pay_s[0:7, l * BLOCK : (l + 1) * BLOCK] = block
        turned = jnp.transpose(rows)
        for p in range(10):
            rows_s[p, l * BLOCK : (l + 1) * BLOCK, :] = jnp.broadcast_to(
                turned[:, p : p + 1], (BLOCK, 128)
            )

    z_wait(zs_i, zr_i, 0)
    for h in range(2):
        top, bottom = zr_i[h, 0:8, :], zr_i[h, 8:16, :]
        for q, tile in enumerate(group_swap((top, bottom, top, bottom))):
            xs_i[h * 4 + q] = tile
    x_start(xs_i, xr_i, 0)
    z_wait(zs_c, zr_c, 1)
    for j in (0, 2):
        for h in range(2):
            tiles = [zr_c[2 * a + h, 8 * b : 8 * b + 8, :] for a in (j, j + 1) for b in (0, 1)]
            for q, tile in enumerate(group_swap(tiles)):
                xs_c[h * 4 + q, 4 * j : 4 * j + 8, :] = tile
    x_start(xs_c, xr_c, 1)
    x_wait(xs_i, xr_i, 0)

    sub8 = iota((8, 128), 0)
    lane8 = iota((8, 128), 1)
    ys = (2 * (8 * ((lane8 // 32) % 2) + sub8) + lane8 // 64).astype(f32)
    xs = []
    for v in range(4):
        first, _ = pair_merge(xr_i[v], xr_i[4 + v])
        xs.append(first + 256.0 * v)
    x_wait(xs_c, xr_c, 1)
    for j in (0, 2):
        for v in range(4):
            first, second = pair_merge(
                xr_c[v, 4 * j : 4 * j + 8, :], xr_c[4 + v, 4 * j : 4 * j + 8, :]
            )
            cot_s[(j * 4 + v) * 8 : (j * 4 + v) * 8 + 8, :] = first
            cot_s[((j + 1) * 4 + v) * 8 : ((j + 1) * 4 + v) * 8 + 8, :] = second

    def bits(p, g):
        return rows_s[p, pl.ds(g, 8, stride=0), :]

    cots = [[cot_s[(j * 4 + v) * 8 : (j * 4 + v) * 8 + 8, :] for v in range(4)] for j in range(4)]

    def ahead(step, carry):
        passing = list(carry[0:4])
        gathered = list(carry[4:8])
        for u in range(UF):
            g = step * UF + u
            mx, my, ca, cb, cc, fade = [bits(p, g) for p in range(6)]
            tint = [bits(6 + j, g) for j in range(4)]
            dy = ys - my
            cross = cb * dy
            base = cc * dy * dy + fade
            for v in range(4):
                dx = xs[v] - mx
                alpha = jnp.exp2((ca * dx + cross) * dx + base)
                weight = alpha * passing[v]
                passing[v] = passing[v] - weight
                shade = tint[0] * cots[0][v]
                for j in range(1, 4):
                    shade = shade + tint[j] * cots[j][v]
                gathered[v] = gathered[v] + weight * shade
                alpha_s[g, v] = alpha
                weight_s[g, v] = weight
                tint_s[g, v] = shade
        return tuple(passing) + tuple(gathered)

    start = tuple(jnp.ones((8, 128), f32) for _ in range(4)) + tuple(
        jnp.zeros((8, 128), f32) for _ in range(4)
    )
    done = lax.fori_loop(0, LIVE // UF, ahead, start)
    passing, gathered = done[0:4], done[4:8]

    for v in range(4):
        xs_2[v], xs_2[4 + v] = pair_merge(gathered[v], passing[v])
    x_start(xs_2, xr_2, 2)
    x_wait(xs_2, xr_2, 2)
    for h in range(2):
        tiles = group_swap([xr_2[h * 4 + q] for q in range(4)])
        for a in range(2):
            for b in range(2):
                zs_2[2 * a + h, 8 * b : 8 * b + 8, :] = tiles[2 * a + b]
    z_start(zs_2, zr_2, 2)
    z_wait(zs_2, zr_2, 2)

    lists = lists_ref[...]
    table = [jnp.concatenate([zr_2[2 * a], zr_2[2 * a + 1]], axis=0) for a in range(2)]
    rowq = iota((32, RAYS), 0)
    picked = [[jnp.zeros((32, RAYS), f32) for _ in range(LISTED)] for _ in range(2)]
    for q in range(4):
        named_q = (rowq % 16) * 8 + (rowq // 16) * 4 + q
        place = rank_s[32 * q : 32 * q + 32, :] + 32 * q
        found = [
            jnp.concatenate([take(table[a], place[:, 0:128]), take(table[a], place[:, 128:256])], axis=1)
            for a in range(2)
        ]
        for k in range(LISTED):
            match = lists[k : k + 1, :] == named_q
            for a in range(2):
                picked[a][k] = jnp.where(match, found[a], picked[a][k])
    entry = [[jnp.sum(picked[a][k], axis=0, keepdims=True) for k in range(LISTED)] for a in range(2)]
    carried = [jnp.ones((1, RAYS), f32)]
    for k in range(LISTED):
        carried.append(carried[k] * entry[1][k])
    behind = [None] * LISTED
    tail = jnp.zeros((1, RAYS), f32)
    for k in reversed(range(LISTED)):
        behind[k] = carried[k] * tail
        tail = entry[0][k] + entry[1][k] * tail

    spot, half, valid = slot_s[0], slot_s[1], slot_s[2]
    sent = [jnp.zeros((32, 128), f32) for _ in range(2)]
    for q in range(4):
        named_q = (rowq % 16) * 8 + (rowq // 16) * 4 + q
        dense = [jnp.zeros((32, RAYS), f32) for _ in range(2)]
        for k in range(LISTED):
            match = lists[k : k + 1, :] == named_q
            dense[0] = jnp.where(match, carried[k], dense[0])
            dense[1] = jnp.where(match, behind[k], dense[1])
        keep = (group == q) & (valid == 1)
        for a in range(2):
            got = jnp.where(half == 1, take(dense[a][:, 128:256], spot), take(dense[a][:, 0:128], spot))
            sent[a] = jnp.where(keep, got, sent[a])
    for a in range(2):
        for h in range(2):
            zs_3[2 * a + h] = sent[a][16 * h : 16 * h + 16, :]
    z_start(zs_3, zr_3, 3)
    z_wait(zs_3, zr_3, 3)
    for h in range(2):
        tiles = [zr_3[2 * a + h, 8 * b : 8 * b + 8, :] for a in range(2) for b in range(2)]
        for q, tile in enumerate(group_swap(tiles)):
            xs_3[h * 4 + q] = tile
    x_start(xs_3, xr_3, 3)
    x_wait(xs_3, xr_3, 3)
    scale, rest = [], []
    for v in range(4):
        first, second = pair_merge(xr_3[v], xr_3[4 + v])
        scale.append(first)
        rest.append(second)
    for j in range(4):
        for v in range(4):
            at = (j * 4 + v) * 8
            cot_s[at : at + 8, :] = cot_s[at : at + 8, :] * scale[v]
    lit = [[cot_s[(j * 4 + v) * 8 : (j * 4 + v) * 8 + 8, :] for v in range(4)] for j in range(4)]

    def back(step, carry):
        behind = list(carry)
        first = (LIVE // UB - 1 - step) * UB
        for u in reversed(range(UB)):
            g = first + u
            mx, my = bits(0, g), bits(1, g)
            dy = ys - my
            total = total_x = total_xx = None
            tints = [None] * 4
            for v in range(4):
                alpha = alpha_s[g, v]
                weight = weight_s[g, v]
                gap = scale[v] * tint_s[g, v] - behind[v]
                behind[v] = behind[v] + alpha * gap
                d = weight * gap
                dx = xs[v] - mx
                d_x = d * dx
                d_xx = d_x * dx
                lights = [weight * lit[j][v] for j in range(4)]
                if v == 0:
                    total, total_x, total_xx, tints = d, d_x, d_xx, lights
                else:
                    total, total_x, total_xx = total + d, total_x + d_x, total_xx + d_xx
                    tints = [s + t for s, t in zip(tints, lights)]
            total_y = total * dy
            sums = [total, total_x, total_xx, total_y, total_y * dy, total_x * dy] + tints
            for p, s in enumerate(sums):
                acc_s[p, 8 * u : 8 * u + 8, :] = s
        for p in range(10):
            folded = acc_s[p, pl.ds(0, 8, stride=8), :]
            for i in range(1, 8):
                folded = folded + acc_s[p, pl.ds(i, 8, stride=8), :]
            red_s[p, pl.ds(pl.multiple_of(first, 8), 8), :] = folded
        return tuple(behind)

    lax.fori_loop(0, LIVE // UB, back, tuple(rest))

    row16 = iota((16, 128), 0)
    moments = jnp.zeros((16, LIVE), f32)
    for p in range(10):
        ones = jnp.where(row16 == p, 1.0, 0.0).astype(bf16)
        whole = red_s[p]
        high = whole.astype(bf16)
        low = (whole - high.astype(f32)).astype(bf16)
        for part in (high, low):
            moments = moments + lax.dot_general(
                ones, part, (((1,), (1,)), ((), ())), preferred_element_type=f32
            )
    s0, sx, sxx, sy, syy, sxy = [moments[p : p + 1] for p in range(6)]
    ga, gb, gc, go = [pay_s[p : p + 1, :] for p in (2, 3, 4, 5)]
    block_row = jnp.concatenate(
        [jnp.full((1, BLOCK), ids[l].astype(f32), f32) for l in range(NLIST)], axis=1
    )
    payload = jnp.concatenate(
        [
            ga * sx + gb * sy,
            gb * sx + gc * sy,
            -0.5 * sxx,
            -sxy,
            -0.5 * syy,
            s0 / go,
            moments[9:10],
            block_row,
            moments[6:9],
            jnp.zeros((5, LIVE), f32),
        ],
        axis=0,
    )
    pay_s[...] = payload

    def y_copy(other):
        return pltpu.make_async_remote_copy(
            src_ref=pay_s,
            dst_ref=pay_r.at[view],
            send_sem=ysend.at[other],
            recv_sem=yrecv.at[view],
            device_id={"tile": other},
        )

    own_copy = pltpu.make_async_copy(pay_s, pay_r.at[view], yrecv.at[view])
    own_copy.start()
    for i in range(NT - 1):
        y_copy((view + 1 + i) % NT).start()
    z_drain(zs_i, zr_i, 0)
    z_drain(zs_c, zr_c, 1)
    z_drain(zs_2, zr_2, 2)
    z_drain(zs_3, zr_3, 3)
    x_drain(xs_i, xr_i, 0)
    x_drain(xs_c, xr_c, 1)
    x_drain(xs_2, xr_2, 2)
    x_drain(xs_3, xr_3, 3)
    own_copy.wait()
    for i in range(NT - 1):
        other = (view + 1 + i) % NT
        pltpu.make_async_remote_copy(
            src_ref=pay_s,
            dst_ref=pay_r.at[other],
            send_sem=ysend.at[other],
            recv_sem=yrecv.at[other],
            device_id={"tile": other},
        ).wait()
    pay_out[...] = pay_r[...]


def expand(pay, har, geo_out, sh_out, tint_s):
    tops = [[pay[v, 0:8, l * BLOCK : (l + 1) * BLOCK] for l in range(NLIST)] for v in range(NT)]
    for b in range(geo_out.shape[1] // BLOCK):
        cols = slice(b * BLOCK, (b + 1) * BLOCK)
        geo = jnp.zeros((8, BLOCK), f32)
        for v in range(NT):
            tint = jnp.zeros((8, BLOCK), f32)
            for l in range(NLIST):
                match = tops[v][l][7:8, :] == float(b)
                geo = geo + jnp.where(match, tops[v][l], 0.0)
                tint = tint + jnp.where(match, pay[v, 8:16, l * BLOCK : (l + 1) * BLOCK], 0.0)
            tint_s[8 * v : 8 * v + 8, cols] = tint
        geo_out[:, cols] = geo[0:7]
    sh_out[...] = lax.dot_general(
        har[:, 0:48], tint_s[...], (((0,), (0,)), ((), ())),
        precision=highest, preferred_element_type=f32,
    )


def body(ray_cot, ray_lists, geometry, sh_coef, view_angles, block_ids, block_counts):
    resident = geometry.shape[1]
    vmem = pl.BlockSpec(memory_space=pltpu.VMEM)
    smem = pl.BlockSpec(memory_space=pltpu.SMEM)
    hbm = pl.BlockSpec(memory_space=pl.ANY)

    def room(*shape):
        return pltpu.VMEM(shape, f32)

    z_pair = lambda n: [room(n, NZ, 128), room(n, NZ, 128)]
    x_pair = lambda n: [room(PLANE, n, 128), room(PLANE, n, 128)]
    payload, harmonics = pl.pallas_call(
        kernel,
        out_shape=(
            jax.ShapeDtypeStruct((NT, 16, LIVE), f32),
            jax.ShapeDtypeStruct((8 * NT, 128), f32),
        ),
        in_specs=[smem, smem, smem, vmem, vmem, hbm, hbm],
        out_specs=(vmem, vmem),
        scratch_shapes=[
            room(7, resident), room(48, resident), room(128, RAYS),
            pltpu.VMEM((128, RAYS), i32), pltpu.VMEM((3, 32, 128), i32),
            *z_pair(2), *z_pair(8), *x_pair(8), *x_pair(16),
            *x_pair(8), *z_pair(4), *z_pair(4), *x_pair(8),
            room(10, LIVE, 128), room(LIVE, 4, 8, 128), room(LIVE, 4, 8, 128),
            room(LIVE, 4, 8, 128), room(10, 64, 128), room(10, LIVE, 128),
            room(128, 128), room(16, LIVE), room(NT, 16, LIVE),
            pltpu.SemaphoreType.DMA((4, NZ)), pltpu.SemaphoreType.DMA((4, NZ)),
            pltpu.SemaphoreType.DMA((4, PLANE)), pltpu.SemaphoreType.DMA((4, PLANE)),
            pltpu.SemaphoreType.DMA((NT,)), pltpu.SemaphoreType.DMA((NT,)),
            pltpu.SemaphoreType.DMA((2,)),
        ],
        compiler_params=pltpu.CompilerParams(collective_id=0, has_side_effects=True),
        name="splat",
    )(
        view_angles, block_ids[0, 0], block_counts[0], ray_cot[:, 0, :],
        jnp.transpose(ray_lists[0]), geometry, sh_coef,
    )
    return pl.pallas_call(
        expand,
        out_shape=(
            jax.ShapeDtypeStruct((7, resident), f32),
            jax.ShapeDtypeStruct((48, resident), f32),
        ),
        in_specs=[vmem, vmem],
        out_specs=(vmem, vmem),
        scratch_shapes=[room(8 * NT, resident)],
        name="expand",
    )(payload, harmonics)


def solution(mesh):
    return jax.shard_map(
        body,
        mesh=mesh,
        in_specs=(
            P(None, "tile", "sub"),
            P("tile", "sub", None),
            P(None, "sub"),
            P(None, "sub"),
            P(),
            P("sub", "tile", None),
            P("sub", "tile"),
        ),
        out_specs=(P(None, "sub"), P(None, "sub")),
        check_vma=False,
    )
```

```python
import jax
import jax.numpy as jnp
from jax import lax
from jax.experimental import pallas as pl
from jax.experimental.pallas import tpu as pltpu
from jax.sharding import PartitionSpec as P

NZ, NX, NC, NT = 16, 4, 2, 4
PLANE = NX * NC
BLOCK, NLIST, LISTED, RAYS = 128, 4, 8, 256
LIVE = NLIST * BLOCK
LOG2E = 1.4426950408889634
f32, i32, bf16 = jnp.float32, jnp.int32, jnp.bfloat16
highest = lax.Precision.HIGHEST
UF, UB = 8, 16


def iota(shape, axis):
    return lax.broadcasted_iota(i32, shape, axis)


def take(table, index):
    return jnp.take_along_axis(table, index, axis=1, mode="promise_in_bounds")


def group_swap(tiles):
    lane = iota((8, 128), 1)
    low = lane < 64
    even = (lane // 32) % 2 == 0
    a, b, c, d = tiles
    a, c = jnp.where(low, a, pltpu.roll(c, 64, 1)), jnp.where(low, pltpu.roll(a, 64, 1), c)
    b, d = jnp.where(low, b, pltpu.roll(d, 64, 1)), jnp.where(low, pltpu.roll(b, 64, 1), d)
    a, b = jnp.where(even, a, pltpu.roll(b, 32, 1)), jnp.where(even, pltpu.roll(a, 96, 1), b)
    c, d = jnp.where(even, c, pltpu.roll(d, 32, 1)), jnp.where(even, pltpu.roll(c, 96, 1), d)
    return a, b, c, d


def pair_merge(first, second):
    low = iota((8, 128), 1) < 64
    return (
        jnp.where(low, first, pltpu.roll(second, 64, 1)),
        jnp.where(low, pltpu.roll(first, 64, 1), second),
    )


def harmonic_rows(angles):
    shape = (8 * NT, 128)
    view = iota(shape, 0) // 8
    row = iota(shape, 1)
    azimuth = jnp.zeros(shape, f32)
    elevation = jnp.zeros(shape, f32)
    for v in range(NT):
        azimuth = jnp.where(view == v, jnp.broadcast_to(angles[0:1, v : v + 1], shape), azimuth)
        elevation = jnp.where(view == v, jnp.broadcast_to(angles[1:2, v : v + 1], shape), elevation)
    x = jnp.cos(elevation) * jnp.cos(azimuth)
    y = jnp.cos(elevation) * jnp.sin(azimuth)
    z = jnp.sin(elevation)
    xx, yy, zz = x * x, y * y, z * z
    terms = [
        0.28209479177387814 * jnp.ones_like(x),
        -0.4886025119029199 * y,
        0.4886025119029199 * z,
        -0.4886025119029199 * x,
        1.0925484305920792 * x * y,
        -1.0925484305920792 * y * z,
        0.31539156525252005 * (2.0 * zz - xx - yy),
        -1.0925484305920792 * x * z,
        0.5462742152960396 * (xx - yy),
        -0.5900435899266435 * y * (3.0 * xx - yy),
        2.890611442640554 * x * y * z,
        -0.4570457994644658 * y * (4.0 * zz - xx - yy),
        0.3731763325901154 * z * (2.0 * zz - 3.0 * xx - 3.0 * yy),
        -0.4570457994644658 * x * (4.0 * zz - xx - yy),
        1.445305721320277 * z * (xx - yy),
        -0.5900435899266435 * x * (xx - 3.0 * yy),
    ]
    out = jnp.zeros(shape, f32)
    for k, term in enumerate(terms):
        out = jnp.where(row // 3 == k, term, out)
    return jnp.where((row % 3 == iota(shape, 0) % 8) & (row < 48), out, 0.0)


def kernel(
    angles_hbm, ids_hbm, counts, ray_cot_hbm, lists_hbm, geo_hbm, sh_hbm,
    pay_out, har_out,
    angles_s, ids_s, ray_cot_s, lists_ref,
    geo_s, sh_s, cum_s, rank_s, slot_s,
    zs_i, zr_i, zs_c, zr_c, xs_i, xr_i, xs_c, xr_c,
    xs_2, xr_2, zs_2, zr_2, zs_3, zr_3, xs_3, xr_3,
    rows_s, alpha_s, weight_s, tint_s, high_s, low_s, red_s, cot_s, pay_s, pay_r,
    zsend, zrecv, xsend, xrecv, ysend, yrecv, lsem,
):
    me = lax.axis_index("sub")
    view = lax.axis_index("tile")
    mz = me // PLANE
    mp = me % PLANE

    def far(i):
        return (mz + 8 + ((i + 1) // 2) * (1 - 2 * (i % 2)) + NZ) % NZ

    barrier = pltpu.get_barrier_semaphore()

    def greet_z(i, c):
        pl.semaphore_signal(barrier, inc=1, device_id={"sub": far(i) * PLANE + mp})
        return c

    def greet_p(i, c):
        pl.semaphore_signal(barrier, inc=1, device_id={"sub": mz * PLANE + (mp + 1 + i) % PLANE})
        return c

    def greet_y(i, c):
        pl.semaphore_signal(barrier, inc=1, device_id={"tile": (view + 1 + i) % NT})
        return c

    lax.fori_loop(0, NZ - 1, greet_z, 0)
    lax.fori_loop(0, PLANE - 1, greet_p, 0)
    lax.fori_loop(0, NT - 1, greet_y, 0)

    fetches = [
        pltpu.make_async_copy(src, dst, lsem.at[n])
        for n, (src, dst) in enumerate(
            [
                (lists_hbm, lists_ref), (ray_cot_hbm, ray_cot_s), (angles_hbm, angles_s),
                (ids_hbm, ids_s), (geo_hbm, geo_s), (sh_hbm, sh_s),
            ]
        )
    ]
    for fetch in fetches:
        fetch.start()
    for fetch in fetches[0:2]:
        fetch.wait()

    def z_copy(src, dst, phase, other):
        return pltpu.make_async_remote_copy(
            src_ref=src.at[:, other, :],
            dst_ref=dst.at[:, mz, :],
            send_sem=zsend.at[phase, other],
            recv_sem=zrecv.at[phase, mz],
            device_id={"sub": other * PLANE + mp},
        )

    def z_start(src, dst, phase):
        pltpu.make_async_copy(src.at[:, mz, :], dst.at[:, mz, :], zrecv.at[phase, mz]).start()

        def go(i, c):
            z_copy(src, dst, phase, far(i)).start()
            return c

        lax.fori_loop(0, NZ - 1, go, 0)

    def z_wait(src, dst, phase):
        pltpu.make_async_copy(src.at[:, mz, :], dst.at[:, mz, :], zrecv.at[phase, mz]).wait()

        def go(i, c):
            other = (mz + 1 + i) % NZ
            pltpu.make_async_remote_copy(
                src_ref=src.at[:, other, :],
                dst_ref=dst.at[:, other, :],
                send_sem=zsend.at[phase, other],
                recv_sem=zrecv.at[phase, other],
                device_id={"sub": other * PLANE + mp},
            ).wait_recv()
            return c

        lax.fori_loop(0, NZ - 1, go, 0)

    def z_drain(src, dst, phase):
        def go(i, c):
            z_copy(src, dst, phase, (mz + 1 + i) % NZ).wait_send()
            return c

        lax.fori_loop(0, NZ - 1, go, 0)

    def x_copy(src, dst, phase, other):
        return pltpu.make_async_remote_copy(
            src_ref=src.at[other],
            dst_ref=dst.at[mp],
            send_sem=xsend.at[phase, other],
            recv_sem=xrecv.at[phase, mp],
            device_id={"sub": mz * PLANE + other},
        )

    def x_start(src, dst, phase):
        pltpu.make_async_copy(src.at[mp], dst.at[mp], xrecv.at[phase, mp]).start()

        def go(i, c):
            x_copy(src, dst, phase, (mp + 1 + i) % PLANE).start()
            return c

        lax.fori_loop(0, PLANE - 1, go, 0)

    def x_wait(src, dst, phase):
        pltpu.make_async_copy(src.at[mp], dst.at[mp], xrecv.at[phase, mp]).wait()

        def go(i, c):
            other = (mp + 1 + i) % PLANE
            pltpu.make_async_remote_copy(
                src_ref=src.at[other],
                dst_ref=dst.at[other],
                send_sem=xsend.at[phase, other],
                recv_sem=xrecv.at[phase, other],
                device_id={"sub": mz * PLANE + other},
            ).wait_recv()
            return c

        lax.fori_loop(0, PLANE - 1, go, 0)

    def x_drain(src, dst, phase):
        def go(i, c):
            x_copy(src, dst, phase, (mp + 1 + i) % PLANE).wait_send()
            return c

        lax.fori_loop(0, PLANE - 1, go, 0)

    lists = lists_ref[...]
    row = iota((128, RAYS), 0)
    named = (row % 16) * 8 + ((row // 16) % 2) * 4 + row // 32
    hit = jnp.zeros((128, RAYS), f32)
    for k in range(LISTED):
        hit = jnp.where(lists[k : k + 1, :] == named, 1.0, hit)
    upper = jnp.where(iota((RAYS, RAYS), 0) <= iota((RAYS, RAYS), 1), 1.0, 0.0).astype(bf16)
    cum = jnp.dot(hit.astype(bf16), upper, preferred_element_type=f32)
    cum_s[...] = cum
    rank_s[...] = jnp.minimum((cum - hit).astype(i32), 31)

    lane = iota((32, 128), 1)
    group = lane // 32
    want = (lane % 32).astype(f32)
    spot = jnp.zeros((32, 128), i32)
    half = jnp.zeros((32, 128), i32)
    valid = jnp.zeros((32, 128), i32)
    for q in range(4):
        left = cum_s[32 * q : 32 * q + 32, 0:128]
        right = cum_s[32 * q : 32 * q + 32, 128:256]
        in_right = left[:, 127:128] <= want
        pos = jnp.zeros((32, 128), i32)
        for step in (64, 32, 16, 8, 4, 2, 1):
            probe = pos + (step - 1)
            seen = jnp.where(in_right, take(right, probe), take(left, probe))
            pos = jnp.where(seen <= want, pos + step, pos)
        here = group == q
        spot = jnp.where(here, pos, spot)
        half = jnp.where(here & in_right, 1, half)
        valid = jnp.where(here & (want < right[:, 127:128]), 1, valid)
    slot_s[0] = spot
    slot_s[1] = half
    slot_s[2] = valid
    index = (spot + 128 * half).astype(f32)
    for h in range(2):
        zs_i[h] = index[16 * h : 16 * h + 16, :]
    for j in range(4):
        left = jnp.broadcast_to(ray_cot_s[j][:, 0:128], (32, 128))
        right = jnp.broadcast_to(ray_cot_s[j][:, 128:256], (32, 128))
        picked = jnp.where(half == 1, take(right, spot), take(left, spot))
        for h in range(2):
            zs_c[2 * j + h] = picked[16 * h : 16 * h + 16, :]

    for fetch in fetches[2:]:
        fetch.wait()
    harmonics = harmonic_rows(angles_s)
    har_out[...] = harmonics
    cot_s[0:32, :] = harmonics
    own = cot_s[pl.ds(pl.multiple_of(view * 8, 8), 8), :]
    for l in range(NLIST):
        chosen = jnp.broadcast_to(ids_s[0][:, l : l + 1], (1, BLOCK))
        block = geo_s[:, 0:BLOCK]
        coef = sh_s[:, 0:BLOCK]
        for b in range(1, geo_s.shape[1] // BLOCK):
            match = chosen == b
            block = jnp.where(match, geo_s[:, b * BLOCK : (b + 1) * BLOCK], block)
            coef = jnp.where(match, sh_s[:, b * BLOCK : (b + 1) * BLOCK], coef)
        colour = 0.5 + jnp.dot(own[:, 0:48], coef, precision=highest)
        live = jnp.full((1, BLOCK), counts[0, 0], i32) > l
        fade = jnp.where(live, jnp.log(block[5:6]) * LOG2E, -1e30)
        rows = jnp.concatenate(
            [
                block[0:2],
                block[2:3] * (-0.5 * LOG2E),
                block[3:4] * (-LOG2E),
                block[4:5] * (-0.5 * LOG2E),
                fade,
                colour[0:3],
                block[6:7],
                jnp.zeros((6, BLOCK), f32),
            ],
            axis=0,
        )
        pay_s[l, 0:7, :] = block
        pay_s[l, 7:8, :] = chosen.astype(f32)
        turned = jnp.transpose(rows)
        for p in range(10):
            rows_s[p, l * BLOCK : (l + 1) * BLOCK, :] = jnp.broadcast_to(
                turned[:, p : p + 1], (BLOCK, 128)
            )

    pl.semaphore_wait(barrier, NZ - 1 + PLANE - 1 + NT - 1)
    z_start(zs_i, zr_i, 0)
    z_start(zs_c, zr_c, 1)

    z_wait(zs_i, zr_i, 0)
    for h in range(2):
        top, bottom = zr_i[h, 0:8, :], zr_i[h, 8:16, :]
        for q, tile in enumerate(group_swap((top, bottom, top, bottom))):
            xs_i[h * 4 + q] = tile
    x_start(xs_i, xr_i, 0)
    z_wait(zs_c, zr_c, 1)
    for j in (0, 2):
        for h in range(2):
            tiles = [zr_c[2 * a + h, 8 * b : 8 * b + 8, :] for a in (j, j + 1) for b in (0, 1)]
            for q, tile in enumerate(group_swap(tiles)):
                xs_c[h * 4 + q, 4 * j : 4 * j + 8, :] = tile
    x_start(xs_c, xr_c, 1)
    x_wait(xs_i, xr_i, 0)

    sub8 = iota((8, 128), 0)
    lane8 = iota((8, 128), 1)
    ys = (2 * (8 * ((lane8 // 32) % 2) + sub8) + lane8 // 64).astype(f32)
    xs = []
    for v in range(4):
        first, _ = pair_merge(xr_i[v], xr_i[4 + v])
        xs.append(first + 256.0 * v)
    x_wait(xs_c, xr_c, 1)
    for j in (0, 2):
        for v in range(4):
            first, second = pair_merge(
                xr_c[v, 4 * j : 4 * j + 8, :], xr_c[4 + v, 4 * j : 4 * j + 8, :]
            )
            cot_s[(j * 4 + v) * 8 : (j * 4 + v) * 8 + 8, :] = first
            cot_s[((j + 1) * 4 + v) * 8 : ((j + 1) * 4 + v) * 8 + 8, :] = second

    def bits(p, g):
        return rows_s[p, pl.ds(g, 8, stride=0), :]

    cots = [[cot_s[(j * 4 + v) * 8 : (j * 4 + v) * 8 + 8, :] for v in range(4)] for j in range(4)]

    def ahead(step, carry):
        passing = list(carry[0:4])
        gathered = list(carry[4:8])
        for u in range(UF):
            g = step * UF + u
            mx, my, ca, cb, cc, fade = [bits(p, g) for p in range(6)]
            tint = [bits(6 + j, g) for j in range(4)]
            dy = ys - my
            cross = cb * dy
            base = cc * dy * dy + fade
            for v in range(4):
                dx = xs[v] - mx
                alpha = jnp.exp2((ca * dx + cross) * dx + base)
                weight = alpha * passing[v]
                passing[v] = passing[v] - weight
                shade = tint[0] * cots[0][v]
                for j in range(1, 4):
                    shade = shade + tint[j] * cots[j][v]
                gathered[v] = gathered[v] + weight * shade
                alpha_s[g, v] = alpha
                weight_s[g, v] = weight
                tint_s[g, v] = shade
        return tuple(passing) + tuple(gathered)

    start = tuple(jnp.ones((8, 128), f32) for _ in range(4)) + tuple(
        jnp.zeros((8, 128), f32) for _ in range(4)
    )
    done = lax.fori_loop(0, LIVE // UF, ahead, start)
    passing, gathered = done[0:4], done[4:8]

    for v in range(4):
        xs_2[v], xs_2[4 + v] = pair_merge(gathered[v], passing[v])
    x_start(xs_2, xr_2, 2)
    x_wait(xs_2, xr_2, 2)
    for h in range(2):
        tiles = group_swap([xr_2[h * 4 + q] for q in range(4)])
        for a in range(2):
            for b in range(2):
                zs_2[2 * a + h, 8 * b : 8 * b + 8, :] = tiles[2 * a + b]
    z_start(zs_2, zr_2, 2)
    z_wait(zs_2, zr_2, 2)

    lists = lists_ref[...]
    table = [jnp.concatenate([zr_2[2 * a], zr_2[2 * a + 1]], axis=0) for a in range(2)]
    rowq = iota((32, RAYS), 0)
    picked = [[jnp.zeros((32, RAYS), f32) for _ in range(LISTED)] for _ in range(2)]
    for q in range(4):
        named_q = (rowq % 16) * 8 + (rowq // 16) * 4 + q
        place = rank_s[32 * q : 32 * q + 32, :] + 32 * q
        found = [
            jnp.concatenate([take(table[a], place[:, 0:128]), take(table[a], place[:, 128:256])], axis=1)
            for a in range(2)
        ]
        for k in range(LISTED):
            match = lists[k : k + 1, :] == named_q
            for a in range(2):
                picked[a][k] = jnp.where(match, found[a], picked[a][k])
    entry = [[jnp.sum(picked[a][k], axis=0, keepdims=True) for k in range(LISTED)] for a in range(2)]
    carried = [jnp.ones((1, RAYS), f32)]
    for k in range(LISTED):
        carried.append(carried[k] * entry[1][k])
    behind = [None] * LISTED
    tail = jnp.zeros((1, RAYS), f32)
    for k in reversed(range(LISTED)):
        behind[k] = carried[k] * tail
        tail = entry[0][k] + entry[1][k] * tail

    spot, half, valid = slot_s[0], slot_s[1], slot_s[2]
    sent = [jnp.zeros((32, 128), f32) for _ in range(2)]
    for q in range(4):
        named_q = (rowq % 16) * 8 + (rowq // 16) * 4 + q
        dense = [jnp.zeros((32, RAYS), f32) for _ in range(2)]
        for k in range(LISTED):
            match = lists[k : k + 1, :] == named_q
            dense[0] = jnp.where(match, carried[k], dense[0])
            dense[1] = jnp.where(match, behind[k], dense[1])
        keep = (group == q) & (valid == 1)
        for a in range(2):
            got = jnp.where(half == 1, take(dense[a][:, 128:256], spot), take(dense[a][:, 0:128], spot))
            sent[a] = jnp.where(keep, got, sent[a])
    for a in range(2):
        for h in range(2):
            zs_3[2 * a + h] = sent[a][16 * h : 16 * h + 16, :]
    z_start(zs_3, zr_3, 3)
    z_wait(zs_3, zr_3, 3)
    for h in range(2):
        tiles = [zr_3[2 * a + h, 8 * b : 8 * b + 8, :] for a in range(2) for b in range(2)]
        for q, tile in enumerate(group_swap(tiles)):
            xs_3[h * 4 + q] = tile
    x_start(xs_3, xr_3, 3)
    x_wait(xs_3, xr_3, 3)
    scale, rest = [], []
    for v in range(4):
        first, second = pair_merge(xr_3[v], xr_3[4 + v])
        scale.append(first)
        rest.append(second)
    for j in range(4):
        for v in range(4):
            at = (j * 4 + v) * 8
            cot_s[at : at + 8, :] = cot_s[at : at + 8, :] * scale[v]
    lit = [[cot_s[(j * 4 + v) * 8 : (j * 4 + v) * 8 + 8, :] for v in range(4)] for j in range(4)]

    def fold(ref, first):
        line = jnp.zeros((8, 128), f32)
        for p in range(10):
            parts = [ref[p, 8 * i : 8 * i + 8, :] for i in range(8)]
            while len(parts) > 1:
                parts = [x + y for x, y in zip(parts[::2], parts[1::2])]
            folded = parts[0]
            line = jnp.where(lane8 == p, jnp.sum(folded, axis=1, keepdims=True), line)
        red_s[pl.ds(pl.multiple_of(first, 8), 8), :] = line

    def y_copy(other, l):
        return pltpu.make_async_remote_copy(
            src_ref=pay_s.at[l],
            dst_ref=pay_r.at[view, l],
            send_sem=ysend.at[other, l],
            recv_sem=yrecv.at[view, l],
            device_id={"tile": other},
        )

    def y_own(l):
        return pltpu.make_async_copy(pay_s.at[l], pay_r.at[view, l], yrecv.at[view, l])

    groups = BLOCK // UB
    state = tuple(rest)
    for l in reversed(range(NLIST)):

        def back(step, carry):
            behind = list(carry)
            first = l * BLOCK + (groups - 1 - step) * UB
            fold(low_s, jnp.minimum(first + UB, LIVE - 8))
            for u in reversed(range(UB)):
                g = first + u
                acc = high_s if u >= 8 else low_s
                mx, my = bits(0, g), bits(1, g)
                dy = ys - my
                total = total_x = total_xx = None
                tints = [None] * 4
                for v in range(4):
                    weight = weight_s[g, v]
                    gap = scale[v] * tint_s[g, v] - behind[v]
                    behind[v] = behind[v] + alpha_s[g, v] * gap
                    d = weight * gap
                    dx = xs[v] - mx
                    d_x = d * dx
                    d_xx = d_x * dx
                    lights = [weight * lit[j][v] for j in range(4)]
                    if v == 0:
                        total, total_x, total_xx, tints = d, d_x, d_xx, lights
                    else:
                        total, total_x, total_xx = total + d, total_x + d_x, total_xx + d_xx
                        tints = [s + t for s, t in zip(tints, lights)]
                total_y = total * dy
                sums = [total, total_x, total_xx, total_y, total_y * dy, total_x * dy] + tints
                for p, s in enumerate(sums):
                    acc[p, pl.ds(u % 8, 8, stride=8), :] = s
                if u == 8:
                    fold(high_s, first + 8)
            return tuple(behind)

        if l == NLIST - 1:
            low_s[...] = jnp.zeros_like(low_s)
        state = lax.fori_loop(0, groups, back, state)
        fold(low_s, l * BLOCK)
        moments = jnp.transpose(red_s[l * BLOCK : (l + 1) * BLOCK, :])
        s0, sx, sxx, sy, syy, sxy = [moments[p : p + 1] for p in range(6)]
        ga, gb, gc, go, chosen = [pay_s[l, p : p + 1, :] for p in (2, 3, 4, 5, 7)]
        pay_s[l] = jnp.concatenate(
            [
                ga * sx + gb * sy,
                gb * sx + gc * sy,
                -0.5 * sxx,
                -sxy,
                -0.5 * syy,
                s0 / go,
                moments[9:10],
                chosen,
                moments[6:9],
                jnp.zeros((5, BLOCK), f32),
            ],
            axis=0,
        )
        y_own(l).start()
        for i in range(NT - 1):
            y_copy((view + 1 + i) % NT, l).start()

    z_drain(zs_i, zr_i, 0)
    z_drain(zs_c, zr_c, 1)
    z_drain(zs_2, zr_2, 2)
    z_drain(zs_3, zr_3, 3)
    x_drain(xs_i, xr_i, 0)
    x_drain(xs_c, xr_c, 1)
    x_drain(xs_2, xr_2, 2)
    x_drain(xs_3, xr_3, 3)
    for l in reversed(range(NLIST)):
        y_own(l).wait()
        for i in range(NT - 1):
            other = (view + 1 + i) % NT
            pltpu.make_async_remote_copy(
                src_ref=pay_s.at[l],
                dst_ref=pay_r.at[other, l],
                send_sem=ysend.at[other, l],
                recv_sem=yrecv.at[other, l],
                device_id={"tile": other},
            ).wait()
    pay_out[...] = pay_r[...]


def expand(pay, har, geo_out, sh_out, tint_s):
    tops = [[pay[v, l, 0:8, :] for l in range(NLIST)] for v in range(NT)]
    for b in range(geo_out.shape[1] // BLOCK):
        cols = slice(b * BLOCK, (b + 1) * BLOCK)
        geo = jnp.zeros((8, BLOCK), f32)
        for v in range(NT):
            tint = jnp.zeros((8, BLOCK), f32)
            for l in range(NLIST):
                match = tops[v][l][7:8, :] == float(b)
                geo = geo + jnp.where(match, tops[v][l], 0.0)
                tint = tint + jnp.where(match, pay[v, l, 8:16, :], 0.0)
            tint_s[8 * v : 8 * v + 8, cols] = tint
        geo_out[:, cols] = geo[0:7]
    sh_out[...] = lax.dot_general(
        har[:, 0:48], tint_s[...], (((0,), (0,)), ((), ())),
        precision=highest, preferred_element_type=f32,
    )


def body(ray_cot, ray_lists, geometry, sh_coef, view_angles, block_ids, block_counts):
    resident = geometry.shape[1]
    vmem = pl.BlockSpec(memory_space=pltpu.VMEM)
    hbm = pl.BlockSpec(memory_space=pl.ANY)

    def room(*shape):
        return pltpu.VMEM(shape, f32)

    z_pair = lambda n: [room(n, NZ, 128), room(n, NZ, 128)]
    x_pair = lambda n: [room(PLANE, n, 128), room(PLANE, n, 128)]
    payload, harmonics = pl.pallas_call(
        kernel,
        out_shape=(
            jax.ShapeDtypeStruct((NT, NLIST, 16, BLOCK), f32),
            jax.ShapeDtypeStruct((8 * NT, 128), f32),
        ),
        in_specs=[hbm, hbm, pl.BlockSpec(memory_space=pltpu.SMEM), hbm, hbm, hbm, hbm],
        out_specs=(vmem, vmem),
        scratch_shapes=[
            room(2, NT), pltpu.VMEM((1, 1, NLIST), i32),
            room(4, 1, RAYS), pltpu.VMEM((LISTED, RAYS), i32),
            room(7, resident), room(48, resident), room(128, RAYS),
            pltpu.VMEM((128, RAYS), i32), pltpu.VMEM((3, 32, 128), i32),
            *z_pair(2), *z_pair(8), *x_pair(8), *x_pair(16),
            *x_pair(8), *z_pair(4), *z_pair(4), *x_pair(8),
            room(10, LIVE, 128), room(LIVE, 4, 8, 128), room(LIVE, 4, 8, 128),
            room(LIVE, 4, 8, 128), room(10, 64, 128), room(10, 64, 128), room(LIVE, 128),
            room(128, 128), room(NLIST, 16, BLOCK), room(NT, NLIST, 16, BLOCK),
            pltpu.SemaphoreType.DMA((4, NZ)), pltpu.SemaphoreType.DMA((4, NZ)),
            pltpu.SemaphoreType.DMA((4, PLANE)), pltpu.SemaphoreType.DMA((4, PLANE)),
            pltpu.SemaphoreType.DMA((NT, NLIST)), pltpu.SemaphoreType.DMA((NT, NLIST)),
            pltpu.SemaphoreType.DMA((7,)),
        ],
        compiler_params=pltpu.CompilerParams(collective_id=0, has_side_effects=True),
        name="splat",
    )(
        jnp.transpose(view_angles), block_ids, block_counts, ray_cot,
        jnp.transpose(ray_lists[0]), geometry, sh_coef,
    )
    return pl.pallas_call(
        expand,
        out_shape=(
            jax.ShapeDtypeStruct((7, resident), f32),
            jax.ShapeDtypeStruct((48, resident), f32),
        ),
        in_specs=[vmem, vmem],
        out_specs=(vmem, vmem),
        scratch_shapes=[room(8 * NT, resident)],
        name="expand",
    )(payload, harmonics)


def solution(mesh):
    return jax.shard_map(
        body,
        mesh=mesh,
        in_specs=(
            P(None, "tile", "sub"),
            P("tile", "sub", None),
            P(None, "sub"),
            P(None, "sub"),
            P(),
            P("sub", "tile", None),
            P("sub", "tile"),
        ),
        out_specs=(P(None, "sub"), P(None, "sub")),
        check_vma=False,
    )
```
